256 devices in a mesh: frame: 16 (over z_hi, y, core), row: 16 (over x, z_lo).
Axes of the slice: x: 4, y: 4, z: 8 (z_hi: 2, z_lo: 4; z = z_hi * 4 + z_lo), core: 2. Of those that a mesh axis runs over, the one named last changes fastest.
Arguments:
- latent: bfloat16 [64, 32, 240, 320], P('frame', 'row'), may hold values from -6 to 6
- gain_one: float32 [320], replicated, may hold values from 0.1 to 1.9
- spatial_weight: bfloat16 [3, 3, 320, 320], replicated, may hold values from -0.109375 to 0.109375
- gain_two: float32 [320], replicated, may hold values from 0.1 to 1.9
- temporal_weight: bfloat16 [3, 320, 320], replicated, may hold values from -0.1875 to 0.1875
- gain_three: float32 [320], replicated, may hold values from 0.1 to 1.9
- query_weight: bfloat16 [320, 320], replicated, as said below
- key_weight: bfloat16 [320, 320], replicated, may hold values from -0.3125 to 0.3125
- value_weight: bfloat16 [320, 320], replicated, may hold values from -0.3125 to 0.3125
- out_weight: bfloat16 [320, 320], replicated, may hold values from -0.3125 to 0.3125
Outputs:
- block_out: float32 [64, 32, 240, 320], P('frame', 'row')
The draws below stay inside these ranges and needn't reach their ends.
Inputs may be any that keep to these rules, and one draw needn't show every extreme that they name: `query_weight`: a projection matrix.
All inputs are finite; a program needn't handle non-finite values.
Results may differ from the reference program's by a relative error of at most 0.012.
The reference program's roundings to bfloat16 on the way (of `act_one`, `act_two`, `normed`, `queries`, `weight` and `attended`) count: a program that leaves them out, or rounds other values in their place, can miss the bound.
Values may be sent and summed in bfloat16 or wider, within the bound.
A program may use at most 128 MiB of HBM per device.

```python
import jax
import jax.numpy as jnp
from jax import lax

C = 320
HEAD_DIM = 64
W = 240
FRAMES = 64
HEIGHT = 32


def draw_query_weight(key, part):
    base_key = jax.random.fold_in(jax.random.fold_in(key, 17), 0)
    matrix = jax.random.normal(base_key, (C, C), jnp.float32) / jnp.sqrt(jnp.float32(C))
    return matrix.astype(jnp.bfloat16)


def block_scale(key, shape, pieces, least, largest):
    level, own = 1.0, jax.random.fold_in(key, 6)
    for position, shards_of in pieces:
        heights = jnp.exp(jax.random.uniform(jax.random.fold_in(own, position), (shards_of,), jnp.float32, least / len(pieces), largest / len(pieces)))
        level = level * jnp.repeat(heights, shape[position] // shards_of).reshape([-1 if axis == position else 1 for axis in range(len(shape))])
    return level


def bell_draw(key, shape, deviation, most, cuts=(), held_as=jnp.bfloat16):
    values = deviation * jax.random.normal(key, shape, jnp.float32)
    if cuts:
        values = values * block_scale(key, shape, cuts, -0.22, 0.18)
    return jnp.clip(values, -most, most).astype(held_as)


def setup_inputs(seed: int = 0) -> dict:
    seeds = jax.random.split(jax.random.key(seed), 11)
    latent = bell_draw(seeds[0], (FRAMES, HEIGHT, W, C), 1.0, 6.0, ((0, 16), (1, 16)))
    gain_one = jnp.clip(1.0 + 0.18 * jax.random.normal(seeds[1], (C,), jnp.float32), 0.1, 1.9)
    spatial_weight = bell_draw(seeds[2], (3, 3, C, C), (9 * C) ** -0.5, 0.109375)
    gain_two = jnp.clip(1.0 + 0.18 * jax.random.normal(seeds[3], (C,), jnp.float32), 0.1, 1.9)
    temporal_weight = bell_draw(seeds[4], (3, C, C), (3 * C) ** -0.5, 0.1875)
    gain_three = jnp.clip(1.0 + 0.18 * jax.random.normal(seeds[5], (C,), jnp.float32), 0.1, 1.9)
    query_weight = draw_query_weight(jax.random.fold_in(seeds[10], 71), 0)
    key_weight = bell_draw(seeds[7], (C, C), C ** -0.5, 0.3125)
    value_weight = bell_draw(seeds[8], (C, C), C ** -0.5, 0.3125)
    out_weight = bell_draw(seeds[9], (C, C), C ** -0.5, 0.3125)
    return dict(latent=latent, gain_one=gain_one, spatial_weight=spatial_weight, gain_two=gain_two, temporal_weight=temporal_weight, gain_three=gain_three, query_weight=query_weight, key_weight=key_weight, value_weight=value_weight, out_weight=out_weight)


def rms_norm(values, gain):
    mean_sq = lax.optimization_barrier(jnp.mean(values * values, axis=-1, keepdims=True))
    return values * lax.rsqrt(mean_sq + 1e-06) * gain

def attend_block(normed, query_weight, key_weight, value_weight):
    frames, pixels, chans = normed.shape
    flat = normed.reshape(-1, chans)
    queries = jnp.dot(flat, query_weight, preferred_element_type=jnp.float32).astype(jnp.bfloat16)
    keys = jnp.dot(flat, key_weight, preferred_element_type=jnp.float32).astype(jnp.bfloat16)
    values = jnp.dot(flat, value_weight, preferred_element_type=jnp.float32).astype(jnp.bfloat16)
    heads = chans // HEAD_DIM
    queries = queries.reshape(frames, pixels, heads, HEAD_DIM).astype(jnp.float32)
    keys = keys.reshape(frames, pixels, heads, HEAD_DIM).astype(jnp.float32)
    values = values.reshape(frames, pixels, heads, HEAD_DIM).astype(jnp.float32)
    scores = jnp.einsum('fphd,gphd->phfg', queries, keys) / jnp.sqrt(jnp.float32(HEAD_DIM))
    peak = lax.optimization_barrier(jnp.max(scores, axis=-1, keepdims=True))
    expo = jnp.exp(scores - peak)
    total = lax.optimization_barrier(jnp.sum(expo, axis=-1))
    weight = expo.astype(jnp.bfloat16).astype(jnp.float32)
    summed = jnp.einsum('phfg,gphd->fphd', weight, values)
    summed = summed / jnp.transpose(total, (2, 0, 1))[..., None]
    return summed.reshape(frames, pixels, chans).astype(jnp.bfloat16)

def reference(latent, gain_one, spatial_weight, gain_two, temporal_weight, gain_three, query_weight, key_weight, value_weight, out_weight):
    frames, height, width, chans = latent.shape
    source = latent.astype(jnp.float32)
    act_one = jax.nn.silu(rms_norm(source, gain_one)).astype(jnp.bfloat16)
    kernel = spatial_weight.astype(jnp.float32)

    def conv_frame(single):
        return lax.conv_general_dilated(single[None].astype(jnp.float32), kernel, (1, 1), ((1, 1), (1, 1)), dimension_numbers=('NHWC', 'HWIO', 'NHWC'))[0]
    spatial = lax.map(conv_frame, act_one)
    hidden_one = source + spatial
    hidden_flat = hidden_one.reshape(frames, height * width, chans)
    act_two = jax.nn.silu(rms_norm(hidden_flat, gain_two)).astype(jnp.bfloat16)
    padded = jnp.pad(act_two, ((1, 1), (0, 0), (0, 0)))
    temporal = jnp.zeros((frames * height * width, chans), jnp.float32)
    for tap in range(3):
        temporal = temporal + jnp.dot(padded[tap:tap + frames].reshape(-1, chans), temporal_weight[tap], preferred_element_type=jnp.float32)
    hidden_two = hidden_flat + temporal.reshape(frames, height * width, chans)
    normed = rms_norm(hidden_two, gain_three).astype(jnp.bfloat16)
    blocks = jnp.transpose(normed.reshape(frames, height, width, chans), (1, 0, 2, 3))
    attended = lax.map(lambda blk: attend_block(blk, query_weight, key_weight, value_weight), blocks)
    attended = jnp.transpose(attended, (1, 0, 2, 3)).reshape(-1, chans)
    mixed = jnp.dot(attended, out_weight, preferred_element_type=jnp.float32)
    result = hidden_two.reshape(-1, chans) + mixed
    return result.reshape(frames, height, width, chans)
```

```python
import jax
import jax.numpy as jnp
from jax import lax
from jax.sharding import PartitionSpec as P

HEAD_DIM = 64


def extended(cells, sides, width):
    for axis, dim in sides:
        count = lax.axis_size(axis)
        ends = count - 1
        head = lax.slice_in_dim(cells, 0, width, axis=dim)
        tail = lax.slice_in_dim(cells, cells.shape[dim] - width, cells.shape[dim], axis=dim)
        cells = jnp.concatenate(
            [
                lax.ppermute(tail, axis, [(i, (i + 1) % count) for i in range(ends)]),
                cells,
                lax.ppermute(head, axis, [((i + 1) % count, i) for i in range(ends)]),
            ],
            axis=dim,
        )
    return cells


def rms_norm(values, gain):
    mean_sq = jnp.mean(values * values, axis=-1, keepdims=True)
    return values * lax.rsqrt(mean_sq + 1e-06) * gain


def project(normed, weight):
    chans = normed.shape[-1]
    flat = jnp.dot(normed.reshape(-1, chans), weight, preferred_element_type=jnp.float32)
    return flat.astype(jnp.bfloat16).reshape(normed.shape[:-1] + (weight.shape[1],))


def attend_heads(queries, keys, values):
    frames, pixels, chans = queries.shape
    heads = chans // HEAD_DIM
    q_split = queries.reshape(frames, pixels, heads, HEAD_DIM)
    k_split = keys.reshape(frames, pixels, heads, HEAD_DIM)
    v_split = values.reshape(frames, pixels, heads, HEAD_DIM)
    scores = jnp.einsum(
        "fphd,gphd->phfg", q_split, k_split, preferred_element_type=jnp.float32
    ) / jnp.sqrt(jnp.float32(HEAD_DIM))
    peak = jnp.max(scores, axis=-1, keepdims=True)
    expo = jnp.exp(scores - peak)
    total = jnp.sum(expo, axis=-1)
    weight = expo.astype(jnp.bfloat16)
    summed = jnp.einsum("phfg,gphd->fphd", weight, v_split, preferred_element_type=jnp.float32)
    summed = summed / jnp.transpose(total, (2, 0, 1))[..., None]
    return summed.reshape(frames, pixels, chans).astype(jnp.bfloat16)


def temporal_mix(padded, temporal_weight, frames):
    chans = padded.shape[-1]
    pixels = padded.shape[1]
    total = jnp.zeros((frames * pixels, chans), jnp.float32)
    for tap in range(3):
        total = total + jnp.dot(
            padded[tap : tap + frames].reshape(-1, chans),
            temporal_weight[tap],
            preferred_element_type=jnp.float32,
        )
    return total.reshape(frames, pixels, chans)


def local(
    latent,
    gain_one,
    spatial_weight,
    gain_two,
    temporal_weight,
    gain_three,
    query_weight,
    key_weight,
    value_weight,
    out_weight,
):
    frames_here, rows_here, width, chans = latent.shape
    source = latent.astype(jnp.float32)
    act_one = jax.nn.silu(rms_norm(source, gain_one)).astype(jnp.bfloat16)
    rimmed = extended(act_one, (("row", 1),), 1)
    spatial = lax.conv_general_dilated(
        rimmed,
        spatial_weight,
        (1, 1),
        ((0, 0), (1, 1)),
        dimension_numbers=("NHWC", "HWIO", "NHWC"),
        preferred_element_type=jnp.float32,
    )
    hidden_one = source + spatial
    pixels = rows_here * width
    hidden_flat = hidden_one.reshape(frames_here, pixels, chans)
    act_two = jax.nn.silu(rms_norm(hidden_flat, gain_two)).astype(jnp.bfloat16)
    padded = extended(act_two, (("frame", 0),), 1)
    temporal = temporal_mix(padded, temporal_weight, frames_here)
    hidden_two = hidden_flat + temporal
    normed = rms_norm(hidden_two, gain_three).astype(jnp.bfloat16)
    groups = lax.axis_size("frame")
    per_group = pixels // groups

    moved = lax.all_to_all(
        normed.reshape(frames_here, groups, per_group, chans), "frame", split_axis=1, concat_axis=0, tiled=True
    )
    moved = moved.reshape(frames_here * groups, per_group, chans)
    attended = attend_heads(
        project(moved, query_weight), project(moved, key_weight), project(moved, value_weight)
    ).reshape(frames_here * groups, 1, per_group, chans)
    returned = lax.all_to_all(attended, "frame", split_axis=0, concat_axis=1, tiled=True)
    mixed = jnp.dot(returned.reshape(-1, chans), out_weight, preferred_element_type=jnp.float32)
    result = hidden_two.reshape(-1, chans) + mixed
    return result.reshape(frames_here, rows_here, width, chans)


def solution(mesh):
    return jax.shard_map(
        local,
        mesh=mesh,
        in_specs=(P("frame", "row", None, None), P(), P(), P(), P(), P(), P(), P(), P(), P()),
        out_specs=P("frame", "row", None, None),
        check_vma=False,
    )
```

```python
import functools

import jax
import jax.numpy as jnp
from jax import lax
from jax.experimental import pallas as pl
from jax.experimental.pallas import tpu as pltpu
from jax.sharding import PartitionSpec as P

MESH = pl.DeviceIdType.MESH
F32 = jnp.float32
BF16 = jnp.bfloat16
C = 320
D = 64
ORDER = (0, 3, 1, 2)


def rms(v, gain):
    mean_sq = jnp.sum(v * v, axis=-1, keepdims=True) * (1.0 / C)
    return v * lax.rsqrt(mean_sq + 1e-06) * gain


def silu(v):
    return v / (1.0 + jnp.exp(-v))


def dot(a, b):
    return jnp.dot(a, b, preferred_element_type=F32)


def main_kernel(
    lat, g1, g2, g3, ws_h, wt_h, wq_h, wk_h, wv_h, wo_h,
    out,
    ws, wt, wq, wk, wv, wo,
    pad, send1, recv1, hid, act, hal, act2, edge, nsend, nrecv,
    qb, kb, vb, ab, asend, arecv, zsend,
    wsem, s1, r1, sx, rx, sf, rf, sn, rn, sa, ra, sz, rz, lsem,
):
    me_f = lax.axis_index("frame")
    me_r = lax.axis_index("row")
    z_hi, j = me_f // 8, me_f % 8
    x, z_lo = me_r // 4, me_r % 4
    z = z_hi * 4 + z_lo

    def dev_z(t):
        return {"frame": (t // 4) * 8 + j, "row": x * 4 + t % 4}

    def dev_x(t):
        return {"frame": me_f, "row": t * 4 + z_lo}

    def dev_j(t):
        return {"frame": z_hi * 8 + t, "row": me_r}

    bar = pltpu.get_barrier_semaphore()
    for k in range(1, 8):
        pl.semaphore_signal(bar, 1, device_id=dev_z((z + k) % 8), device_id_type=MESH)
        pl.semaphore_signal(bar, 1, device_id=dev_j((j + k) % 8), device_id_type=MESH)
    for k in (1, 3):
        pl.semaphore_signal(bar, 1, device_id=dev_x((x + k) % 4), device_id_type=MESH)

    loads = [
        pltpu.make_async_copy(a, b, wsem.at[n])
        for n, (a, b) in enumerate(
            ((ws_h, ws), (wt_h, wt), (wq_h, wq), (wk_h, wk), (wv_h, wv), (wo_h, wo))
        )
    ]
    for cp in loads:
        cp.start()

    def remote(src, dst, ss, rs, dev):
        return pltpu.make_async_remote_copy(src, dst, ss, rs, device_id=dev, device_id_type=MESH)

    def z1(k, i):
        t = (z + k) % 8
        return remote(send1.at[t, i], recv1.at[z, i], s1.at[k, i], r1.at[k, i], dev_z(t))

    pad[0:8] = jnp.zeros((8, 2 * C), F32)
    pad[248:256] = jnp.zeros((8, 2 * C), F32)
    for n, i in enumerate(ORDER):
        pad[8:248, 0:C] = lat[i, 0].astype(F32)
        pad[8:248, C : 2 * C] = lat[i, 1].astype(F32)

        for t in range(8):
            send1[t, i] = pad[7 + 30 * t : 39 + 30 * t, :].astype(BF16)
        if n == 0:
            pl.semaphore_wait(bar, 16)
        for k in range(1, 8):
            z1(k, i).start()
        recv1[z, i] = send1[z, i]

    def hx(s, side):
        t = (x + (3 if side else 1)) % 4
        row = 1 if side else 8
        return remote(
            act.at[s, :, row], hal.at[s, side], sx.at[s, side], rx.at[s, side], dev_x(t)
        )

    def hf(side):
        t = (j + (7 if side else 1)) % 8
        slot = 1 if side else 4
        return remote(act2.at[:, slot], edge.at[side], sf.at[side], rf.at[side], dev_j(t))

    def activate(s, i):
        for k in range(1, 8):
            src = (z + 8 - k) % 8
            remote(send1.at[src, i], recv1.at[src, i], s1.at[k, i], r1.at[k, i], dev_z(src)).wait_recv()

        def one(q, _):
            grp, zl = q // 4, q % 4
            both = recv1[q, i].astype(F32)
            for r in range(2):
                v = both[:, r * C : (r + 1) * C]
                hid[grp * 4 + i, 2 * zl + r] = v
                act[s, grp, 2 * zl + r + 1] = silu(rms(v, g1[...])).astype(BF16)
            return 0

        lax.fori_loop(0, 8, one, 0)
        hx(s, 0).start()
        hx(s, 1).start()

    def convolve(s, i):
        for side in range(2):
            hx(s, side).wait_recv()
        top = hal[s, 0]
        bot = hal[s, 1]
        act[s, :, 0] = jnp.where(x > 0, top, jnp.zeros_like(top))
        act[s, :, 9] = jnp.where(x < 3, bot, jnp.zeros_like(bot))

        def one(grp, _):
            ys = []
            for dx in range(3):
                y = None
                for dy in range(3):
                    a = act[s, grp, dy : dy + 8].reshape(256, C)
                    m = dot(a, ws[dy, dx])
                    y = m if y is None else y + m
                ys.append(y)
            h = hid[grp * 4 + i].reshape(256, C) + ys[1]
            h = h + pltpu.roll(ys[0], 1, 0) + pltpu.roll(ys[2], 255, 0)
            hid[grp * 4 + i] = h.reshape(8, 32, C)
            act2[grp, 1 + i] = silu(rms(h, g2[...])).astype(BF16).reshape(8, 32, C)
            return 0

        lax.fori_loop(0, 2, one, 0)
        if i == 3:
            hf(0).start()
        if i == 0:
            hf(1).start()

    for s, i in enumerate(ORDER):
        activate(s, i)
        if s == 1:
            loads[0].wait()
        if s > 0:
            convolve(s - 1, ORDER[s - 1])
    convolve(3, ORDER[3])

    hf(0).wait_recv()
    hf(1).wait_recv()
    zero = jnp.zeros((8, 32, C), BF16)
    first, last = j == 0, j == 7
    act2[0, 0] = jnp.where(first, zero, edge[0, 0])
    act2[1, 0] = jnp.where(first, edge[0, 0], edge[0, 1])
    act2[0, 5] = jnp.where(last, edge[1, 1], edge[1, 0])
    act2[1, 5] = jnp.where(last, zero, edge[1, 1])
    loads[1].wait()

    def na(d):
        t = (j + d) % 8
        return remote(nsend.at[t], nrecv.at[j], sn.at[d], rn.at[d], dev_j(t))

    def temporal(k, _):
        r = (j + 1 + k) % 8
        total = None
        for t in range(3):
            a = act2[:, t : t + 4, r].reshape(256, C)
            m = dot(a, wt[t])
            total = m if total is None else total + m
        h = hid[:, r].reshape(256, C) + total
        hid[:, r] = h.reshape(8, 32, C)
        nsend[r] = rms(h, g3[...]).astype(BF16).reshape(8, 32, C)

        @pl.when(k < 7)
        def _():
            na(k + 1).start()

        return 0

    lax.fori_loop(0, 8, temporal, 0)
    nrecv[j] = nsend[j]
    for n in (2, 3, 4, 5):
        loads[n].wait()

    def project(d, _):
        src = (j + 8 - d) % 8

        @pl.when(d > 0)
        def _():
            remote(nsend.at[src], nrecv.at[src], sn.at[d], rn.at[d], dev_j(src)).wait_recv()

        a = nrecv[src].reshape(256, C)
        rows = pl.ds(pl.multiple_of(src * 256, 256), 256)
        for w, buf, scale in ((wq, qb, 0.125), (wk, kb, None), (wv, vb, None)):
            y = dot(a, w[...]).astype(BF16).astype(F32)
            y = y if scale is None else y * scale
            buf[0, rows, :] = y[:, 0:128]
            buf[1, rows, :] = y[:, 128:256]
            buf[2, rows, 0:D] = y[:, 256:320]
        return 0

    lax.fori_loop(0, 8, project, 0)

    low = lax.broadcasted_iota(jnp.int32, (64, 128), 1) < D

    def softmax_av(q, k, v):
        s = lax.dot_general(q, k, (((1,), (1,)), ((), ())), preferred_element_type=F32)
        e = jnp.exp(s - jnp.max(s, axis=-1, keepdims=True))
        tot = jnp.sum(e, axis=-1, keepdims=True)
        return dot(e.astype(BF16), v) / tot

    def pixel(p, _):
        rows = pl.ds(p, 64, stride=32)
        zq = jnp.zeros((64, 128), BF16)
        for hp in range(2):
            q = qb[hp, rows, :].astype(BF16)
            k = kb[hp, rows, :].astype(BF16)
            v = vb[hp, rows, :].astype(BF16)
            stacked = jnp.concatenate([jnp.where(low, q, zq), jnp.where(low, zq, q)], axis=0)
            o = softmax_av(stacked, k, v)
            ab[hp, rows, :] = jnp.where(low, o[:64], o[64:])
        q = qb[2, rows, :][:, :D].astype(BF16)
        k = kb[2, rows, :][:, :D].astype(BF16)
        v = vb[2, rows, :].astype(BF16)
        ab[2, rows, :] = softmax_av(q, k, v)
        return 0

    def aa(d, c):
        t = (j + d) % 8
        cols = pl.ds(c * 16, 16)
        return remote(asend.at[c, t], arecv.at[j, :, cols], sa.at[c, d], ra.at[c, d], dev_j(t))

    for c in range(2):
        lax.fori_loop(1 if c == 0 else 16, 16 if c == 0 else 31, pixel, 0)

        def gather(t, _):
            rows = pl.ds(pl.multiple_of(t * 256, 256), 256)
            full = jnp.concatenate([ab[0, rows, :], ab[1, rows, :], ab[2, rows, 0:D]], axis=-1)
            asend[c, t] = full.reshape(8, 32, C)[:, c * 16 : c * 16 + 16].astype(BF16)
            return 0

        lax.fori_loop(0, 8, gather, 0)
        for d in range(1, 8):
            aa(d, c).start()
        arecv[j, :, c * 16 : c * 16 + 16] = asend[c, j]

    for c in range(2):
        for d in range(1, 8):
            src = (j + 8 - d) % 8
            cols = pl.ds(c * 16, 16)
            remote(
                asend.at[c, src], arecv.at[src, :, cols], sa.at[c, d], ra.at[c, d], dev_j(src)
            ).wait_recv()

    def z2(k, i):
        t = (z + k) % 8
        return remote(zsend.at[t, i], out.at[z, i], sz.at[k, i], rz.at[k, i], dev_z(t))

    own = []
    for i in range(4):

        def finish(grp, _):
            a = arecv[:, grp * 4 + i].reshape(256, C)
            res = hid[grp * 4 + i].reshape(256, C) + dot(a, wo[...])
            res = res.reshape(4, 2, 32, C)
            for zl in range(4):
                zsend[grp * 4 + zl, i] = jnp.concatenate([res[zl, 0], res[zl, 1]], axis=-1).astype(BF16)
            return 0

        lax.fori_loop(0, 2, finish, 0)
        for k in range(1, 8):
            z2(k, i).start()
        cp = pltpu.make_async_copy(zsend.at[z, i], out.at[z, i], lsem.at[i])
        cp.start()
        own.append(cp)

    for i in range(4):
        own[i].wait()
        for k in range(1, 8):
            src = (z + 8 - k) % 8
            z1(k, i).wait_send()
            z2(k, i).wait_send()
            remote(zsend.at[src, i], out.at[src, i], sz.at[k, i], rz.at[k, i], dev_z(src)).wait_recv()
    for s in range(4):
        for side in range(2):
            hx(s, side).wait_send()
    for side in range(2):
        hf(side).wait_send()
    for d in range(1, 8):
        na(d).wait_send()
        for c in range(2):
            aa(d, c).wait_send()


def last_kernel(parts, out, tmp):
    for t in range(8):
        tmp[t] = parts[t, 0].astype(F32)
        both = tmp[t, 1:31, :]
        out[0, 0, 30 * t : 30 * t + 30, :] = both[:, 0:C]
        out[0, 1, 30 * t : 30 * t + 30, :] = both[:, C : 2 * C]


def local(latent, g1, ws, g2, wt, g3, wq, wk, wv, wo):
    vm = pl.BlockSpec(memory_space=pltpu.VMEM)
    anyspace = pl.BlockSpec(memory_space=pl.ANY)
    dma = pltpu.SemaphoreType.DMA
    parts = pl.pallas_call(
        main_kernel,
        out_shape=jax.ShapeDtypeStruct((8, 4, 32, 2 * C), BF16),
        in_specs=[vm] * 4 + [anyspace] * 6,
        out_specs=anyspace,
        scratch_shapes=[
            pltpu.VMEM((3, 3, C, C), BF16),
            pltpu.VMEM((3, C, C), BF16),
            pltpu.VMEM((C, C), BF16),
            pltpu.VMEM((C, C), BF16),
            pltpu.VMEM((C, C), BF16),
            pltpu.VMEM((C, C), BF16),
            pltpu.VMEM((256, 2 * C), F32),
            pltpu.VMEM((8, 4, 32, 2 * C), BF16),
            pltpu.VMEM((8, 4, 32, 2 * C), BF16),
            pltpu.VMEM((8, 8, 32, C), F32),
            pltpu.VMEM((4, 2, 10, 32, C), BF16),
            pltpu.VMEM((4, 2, 2, 32, C), BF16),
            pltpu.VMEM((2, 6, 8, 32, C), BF16),
            pltpu.VMEM((2, 2, 8, 32, C), BF16),
            pltpu.VMEM((8, 8, 32, C), BF16),
            pltpu.VMEM((8, 8, 32, C), BF16),
            pltpu.VMEM((3, 2048, 128), F32),
            pltpu.VMEM((3, 2048, 128), F32),
            pltpu.VMEM((3, 2048, 128), F32),
            pltpu.VMEM((3, 2048, 128), F32),
            pltpu.VMEM((2, 8, 8, 16, C), BF16),
            pltpu.VMEM((8, 8, 32, C), BF16),
            pltpu.VMEM((8, 4, 32, 2 * C), BF16),
            dma((6,)),
            dma((8, 4)), dma((8, 4)),
            dma((4, 2)), dma((4, 2)),
            dma((2,)), dma((2,)),
            dma((8,)), dma((8,)),
            dma((2, 8)), dma((2, 8)),
            dma((8, 4)), dma((8, 4)),
            dma((4,)),
        ],
        compiler_params=pltpu.CompilerParams(
            collective_id=0, has_side_effects=True, vmem_limit_bytes=60 * 1024 * 1024
        ),
        name="block",
    )(latent, g1.reshape(1, C), g2.reshape(1, C), g3.reshape(1, C), ws, wt, wq, wk, wv, wo)
    return pl.pallas_call(
        last_kernel,
        grid=(4,),
        out_shape=jax.ShapeDtypeStruct((4, 2, 240, C), F32),
        in_specs=[pl.BlockSpec((8, 1, 32, 2 * C), lambda i: (0, i, 0, 0))],
        out_specs=pl.BlockSpec((1, 2, 240, C), lambda i: (i, 0, 0, 0)),
        scratch_shapes=[pltpu.VMEM((8, 32, 2 * C), F32)],
        name="assemble",
    )(parts)


def solution(mesh):
    return jax.shard_map(
        local,
        mesh=mesh,
        in_specs=(P("frame", "row", None, None),) + (P(),) * 9,
        out_specs=P("frame", "row", None, None),
        check_vma=False,
    )
```

```python
import functools

import jax
import jax.numpy as jnp
from jax import lax
from jax.experimental import pallas as pl
from jax.experimental.pallas import tpu as pltpu
from jax.sharding import PartitionSpec as P

MESH = pl.DeviceIdType.MESH
F32 = jnp.float32
BF16 = jnp.bfloat16
C = 320
D = 64
ORDER = (0, 3, 1, 2)


def rms(v, gain):
    mean_sq = jnp.sum(v * v, axis=-1, keepdims=True) * (1.0 / C)
    return v * lax.rsqrt(mean_sq + 1e-06) * gain


def silu(v):
    return v / (1.0 + jnp.exp(-v))


def dot(a, b):
    return jnp.dot(a, b, preferred_element_type=F32)


def main_kernel(
    lat, g1, g2, g3, ws_h, wt_h, wq_h, wk_h, wv_h, wo_h,
    out,
    ws, wt, wq, wk, wv, wo,
    pad, send1, recv1, hid, act, hal, act2, edge, nsend, nrecv,
    qb, kb, vb, ab, asend, arecv, zsend,
    wsem, s1, r1, sx, rx, sf, rf, sn, rn, sa, ra, sz, rz, lsem,
):
    me_f = lax.axis_index("frame")
    me_r = lax.axis_index("row")
    z_hi, j = me_f // 8, me_f % 8
    x, z_lo = me_r // 4, me_r % 4
    z = z_hi * 4 + z_lo

    def dev_z(t):
        return {"frame": (t // 4) * 8 + j, "row": x * 4 + t % 4}

    def dev_x(t):
        return {"frame": me_f, "row": t * 4 + z_lo}

    def dev_j(t):
        return {"frame": z_hi * 8 + t, "row": me_r}

    bar = pltpu.get_barrier_semaphore()
    for k in range(1, 8):
        pl.semaphore_signal(bar, 1, device_id=dev_z((z + k) % 8), device_id_type=MESH)
        pl.semaphore_signal(bar, 1, device_id=dev_j((j + k) % 8), device_id_type=MESH)
    for k in (1, 3):
        pl.semaphore_signal(bar, 1, device_id=dev_x((x + k) % 4), device_id_type=MESH)

    loads = [
        pltpu.make_async_copy(a, b, wsem.at[n])
        for n, (a, b) in enumerate(
            ((ws_h, ws), (wt_h, wt), (wq_h, wq), (wk_h, wk), (wv_h, wv), (wo_h, wo))
        )
    ]
    for cp in loads:
        cp.start()

    def remote(src, dst, ss, rs, dev):
        return pltpu.make_async_remote_copy(src, dst, ss, rs, device_id=dev, device_id_type=MESH)

    def z1(k, i):
        t = (z + k) % 8
        return remote(send1.at[t, i], recv1.at[z, i], s1.at[k, i], r1.at[k, i], dev_z(t))

    pad[0:8] = jnp.zeros((8, 2 * C), F32)
    pad[248:256] = jnp.zeros((8, 2 * C), F32)
    for n, i in enumerate(ORDER):
        pad[8:248, 0:C] = lat[i, 0].astype(F32)
        pad[8:248, C : 2 * C] = lat[i, 1].astype(F32)

        for t in range(8):
            send1[t, i] = pad[7 + 30 * t : 39 + 30 * t, :].astype(BF16)
        if n == 0:
            pl.semaphore_wait(bar, 16)
        for k in range(1, 8):
            z1(k, i).start()
        recv1[z, i] = send1[z, i]

    def hx(s, side):
        t = (x + (3 if side else 1)) % 4
        row = 1 if side else 8
        return remote(
            act.at[s, :, row], hal.at[s, side], sx.at[s, side], rx.at[s, side], dev_x(t)
        )

    def hf(side):
        t = (j + (7 if side else 1)) % 8
        slot = 1 if side else 4
        return remote(act2.at[:, :, slot], edge.at[side], sf.at[side], rf.at[side], dev_j(t))

    def activate(s, i):
        for k in range(1, 8):
            src = (z + 8 - k) % 8
            remote(send1.at[src, i], recv1.at[src, i], s1.at[k, i], r1.at[k, i], dev_z(src)).wait_recv()

        def one(q, _):
            grp, zl = q // 4, q % 4
            both = recv1[q, i].astype(F32)
            for r in range(2):
                v = both[:, r * C : (r + 1) * C]
                for c in range(2):
                    hid[c, grp * 4 + i, 2 * zl + r] = v[c * 16 : c * 16 + 16]
                act[s, grp, 2 * zl + r + 1] = silu(rms(v, g1[...])).astype(BF16)
            return 0

        lax.fori_loop(0, 8, one, 0)
        hx(s, 0).start()
        hx(s, 1).start()

    def convolve(s, i):
        for side in range(2):
            hx(s, side).wait_recv()
        top = hal[s, 0]
        bot = hal[s, 1]
        act[s, :, 0] = jnp.where(x > 0, top, jnp.zeros_like(top))
        act[s, :, 9] = jnp.where(x < 3, bot, jnp.zeros_like(bot))

        def one(grp, _):
            ys = []
            for dx in range(3):
                y = None
                for dy in range(3):
                    a = act[s, grp, dy : dy + 8].reshape(256, C)
                    m = dot(a, ws[dy, dx])
                    y = m if y is None else y + m
                ys.append(y)
            y = ys[1] + pltpu.roll(ys[0], 1, 0) + pltpu.roll(ys[2], 255, 0)
            y = y.reshape(8, 32, C)
            for c in range(2):
                h = hid[c, grp * 4 + i] + y[:, c * 16 : c * 16 + 16]
                hid[c, grp * 4 + i] = h
                act2[c, grp, 1 + i] = silu(rms(h, g2[...])).astype(BF16)
            return 0

        lax.fori_loop(0, 2, one, 0)
        if i == 3:
            hf(0).start()
        if i == 0:
            hf(1).start()

    for s, i in enumerate(ORDER):
        activate(s, i)
        if s == 1:
            loads[0].wait()
        if s > 0:
            convolve(s - 1, ORDER[s - 1])
    convolve(3, ORDER[3])

    hf(0).wait_recv()
    hf(1).wait_recv()
    zero = jnp.zeros((8, 16, C), BF16)
    first, last = j == 0, j == 7
    for c in range(2):
        act2[c, 0, 0] = jnp.where(first, zero, edge[0, c, 0])
        act2[c, 1, 0] = jnp.where(first, edge[0, c, 0], edge[0, c, 1])
        act2[c, 0, 5] = jnp.where(last, edge[1, c, 1], edge[1, c, 0])
        act2[c, 1, 5] = jnp.where(last, zero, edge[1, c, 1])
    loads[1].wait()

    def na(c, d):
        t = (j + d) % 8
        return remote(nsend.at[c, t], nrecv.at[c, j], sn.at[c, d], rn.at[c, d], dev_j(t))

    def temporal(c, kk):
        pair = ((j + 1 + 2 * kk) % 8, (j + 2 + 2 * kk) % 8)
        total = None
        for t in range(3):
            a = jnp.concatenate([act2[c, :, t : t + 4, r].reshape(128, C) for r in pair], axis=0)
            m = dot(a, wt[t])
            total = m if total is None else total + m
        for n, r in enumerate(pair):
            h = hid[c, :, r].reshape(128, C) + total[n * 128 : n * 128 + 128]
            hid[c, :, r] = h.reshape(8, 16, C)
            nsend[c, r] = rms(h, g3[...]).astype(BF16).reshape(8, 16, C)
            if 1 + 2 * kk + n < 8:
                na(c, 1 + 2 * kk + n).start()

    for c in range(2):
        for kk in range(4):
            temporal(c, kk)
        nrecv[c, j] = nsend[c, j]
    for n in (2, 3, 4, 5):
        loads[n].wait()

    def project(c):
        for n in range(4):
            pair = []
            for d in (2 * n, 2 * n + 1):
                src = (j + 8 - d) % 8
                if d > 0:
                    remote(
                        nsend.at[c, src], nrecv.at[c, src], sn.at[c, d], rn.at[c, d], dev_j(src)
                    ).wait_recv()
                pair.append(src)
            a = jnp.concatenate([nrecv[c, src].reshape(128, C) for src in pair], axis=0)
            for w, buf, scale in ((wq, qb, 0.125), (wk, kb, None), (wv, vb, None)):
                y = dot(a, w[...]).astype(BF16).astype(F32)
                y = y if scale is None else y * scale
                for m, src in enumerate(pair):
                    rows = pl.ds(pl.multiple_of(c * 1024 + src * 128, 128), 128)
                    part = y[m * 128 : m * 128 + 128]
                    buf[0, rows, :] = part[:, 0:128]
                    buf[1, rows, :] = part[:, 128:256]
                    buf[2, rows, 0:D] = part[:, 256:320]

    low = lax.broadcasted_iota(jnp.int32, (64, 128), 1) < D

    def softmax_av(q, k, v):
        s = lax.dot_general(q, k, (((1,), (1,)), ((), ())), preferred_element_type=F32)
        e = jnp.exp(s - jnp.max(s, axis=-1, keepdims=True))
        tot = jnp.sum(e, axis=-1, keepdims=True)
        return dot(e.astype(BF16), v) * (1.0 / tot)

    def pixel(c, p):
        rows = pl.ds(c * 1024 + p, 64, stride=16)
        zq = jnp.zeros((64, 128), BF16)
        for hp in range(2):
            q = qb[hp, rows, :].astype(BF16)
            k = kb[hp, rows, :].astype(BF16)
            v = vb[hp, rows, :].astype(BF16)
            stacked = jnp.concatenate([jnp.where(low, q, zq), jnp.where(low, zq, q)], axis=0)
            o = softmax_av(stacked, k, v)
            ab[hp, rows, :] = jnp.where(low, o[:64], o[64:])
        q = qb[2, rows, :][:, :D].astype(BF16)
        k = kb[2, rows, :][:, :D].astype(BF16)
        v = vb[2, rows, :].astype(BF16)
        ab[2, rows, :] = softmax_av(q, k, v)

    def aa(c, d):
        t = (j + d) % 8
        return remote(asend.at[c, t], arecv.at[c, j], sa.at[c, d], ra.at[c, d], dev_j(t))

    def attend(c):
        def five(n, _):
            for m in range(5):
                pixel(c, 1 - c + n * 5 + m)
            return 0

        lax.fori_loop(0, 3, five, 0)

        def gather(t, _):
            rows = pl.ds(pl.multiple_of(c * 1024 + t * 128, 128), 128)
            full = jnp.concatenate([ab[0, rows, :], ab[1, rows, :], ab[2, rows, 0:D]], axis=-1)
            asend[c, t] = full.astype(BF16).reshape(8, 16, C)
            return 0

        lax.fori_loop(0, 8, gather, 0)
        for d in range(1, 8):
            aa(c, d).start()
        arecv[c, j] = asend[c, j]

    def z2(c, k, i):
        t = (z + k) % 8
        return remote(zsend.at[c, t, i], out.at[c, z, i], sz.at[c, k, i], rz.at[c, k, i], dev_z(t))

    def finish(c):
        for d in range(1, 8):
            src = (j + 8 - d) % 8
            remote(asend.at[c, src], arecv.at[c, src], sa.at[c, d], ra.at[c, d], dev_j(src)).wait_recv()
        for i in range(4):
            a = jnp.concatenate([arecv[c, :, g * 4 + i].reshape(128, C) for g in range(2)], axis=0)
            mixed = dot(a, wo[...])
            for g in range(2):
                res = hid[c, g * 4 + i] + mixed[g * 128 : g * 128 + 128].reshape(8, 16, C)
                for zl in range(4):
                    both = jnp.concatenate([res[2 * zl], res[2 * zl + 1]], axis=-1)
                    zsend[c, g * 4 + zl, i] = both.astype(BF16)
            for k in range(1, 8):
                z2(c, k, i).start()
        cp = pltpu.make_async_copy(zsend.at[c, z], out.at[c, z], lsem.at[c])
        cp.start()
        return cp

    project(0)
    attend(0)
    project(1)
    attend(1)
    own = [finish(0), finish(1)]

    for c in range(2):
        own[c].wait()
        for i in range(4):
            for k in range(1, 8):
                src = (z + 8 - k) % 8
                z2(c, k, i).wait_send()
                remote(
                    zsend.at[c, src, i], out.at[c, src, i], sz.at[c, k, i], rz.at[c, k, i], dev_z(src)
                ).wait_recv()
        for d in range(1, 8):
            na(c, d).wait_send()
            aa(c, d).wait_send()
    for i in range(4):
        for k in range(1, 8):
            z1(k, i).wait_send()
    for s in range(4):
        for side in range(2):
            hx(s, side).wait_send()
    for side in range(2):
        hf(side).wait_send()


def last_kernel(parts, out, tmp):
    for t in range(8):
        tmp[t, 0:16] = parts[0, t, 0].astype(F32)
        tmp[t, 16:32] = parts[1, t, 0].astype(F32)
        both = tmp[t, 1:31, :]
        out[0, 0, 30 * t : 30 * t + 30, :] = both[:, 0:C]
        out[0, 1, 30 * t : 30 * t + 30, :] = both[:, C : 2 * C]


def local(latent, g1, ws, g2, wt, g3, wq, wk, wv, wo):
    vm = pl.BlockSpec(memory_space=pltpu.VMEM)
    anyspace = pl.BlockSpec(memory_space=pl.ANY)
    dma = pltpu.SemaphoreType.DMA
    parts = pl.pallas_call(
        main_kernel,
        out_shape=jax.ShapeDtypeStruct((2, 8, 4, 16, 2 * C), BF16),
        in_specs=[vm] * 4 + [anyspace] * 6,
        out_specs=anyspace,
        scratch_shapes=[
            pltpu.VMEM((3, 3, C, C), BF16),
            pltpu.VMEM((3, C, C), BF16),
            pltpu.VMEM((C, C), BF16),
            pltpu.VMEM((C, C), BF16),
            pltpu.VMEM((C, C), BF16),
            pltpu.VMEM((C, C), BF16),
            pltpu.VMEM((256, 2 * C), F32),
            pltpu.VMEM((8, 4, 32, 2 * C), BF16),
            pltpu.VMEM((8, 4, 32, 2 * C), BF16),
            pltpu.VMEM((2, 8, 8, 16, C), F32),
            pltpu.VMEM((4, 2, 10, 32, C), BF16),
            pltpu.VMEM((4, 2, 2, 32, C), BF16),
            pltpu.VMEM((2, 2, 6, 8, 16, C), BF16),
            pltpu.VMEM((2, 2, 2, 8, 16, C), BF16),
            pltpu.VMEM((2, 8, 8, 16, C), BF16),
            pltpu.VMEM((2, 8, 8, 16, C), BF16),
            pltpu.VMEM((3, 2048, 128), F32),
            pltpu.VMEM((3, 2048, 128), F32),
            pltpu.VMEM((3, 2048, 128), F32),
            pltpu.VMEM((3, 2048, 128), F32),
            pltpu.VMEM((2, 8, 8, 16, C), BF16),
            pltpu.VMEM((2, 8, 8, 16, C), BF16),
            pltpu.VMEM((2, 8, 4, 16, 2 * C), BF16),
            dma((6,)),
            dma((8, 4)), dma((8, 4)),
            dma((4, 2)), dma((4, 2)),
            dma((2,)), dma((2,)),
            dma((2, 8)), dma((2, 8)),
            dma((2, 8)), dma((2, 8)),
            dma((2, 8, 4)), dma((2, 8, 4)),
            dma((2,)),
        ],
        compiler_params=pltpu.CompilerParams(
            collective_id=0, has_side_effects=True, vmem_limit_bytes=60 * 1024 * 1024
        ),
        name="block",
    )(latent, g1.reshape(1, C), g2.reshape(1, C), g3.reshape(1, C), ws, wt, wq, wk, wv, wo)
    return pl.pallas_call(
        last_kernel,
        grid=(4,),
        out_shape=jax.ShapeDtypeStruct((4, 2, 240, C), F32),
        in_specs=[pl.BlockSpec((2, 8, 1, 16, 2 * C), lambda i: (0, 0, i, 0, 0))],
        out_specs=pl.BlockSpec((1, 2, 240, C), lambda i: (i, 0, 0, 0)),
        scratch_shapes=[pltpu.VMEM((8, 32, 2 * C), F32)],
        name="assemble",
    )(parts)


def solution(mesh):
    return jax.shard_map(
        local,
        mesh=mesh,
        in_specs=(P("frame", "row", None, None),) + (P(),) * 9,
        out_specs=P("frame", "row", None, None),
        check_vma=False,
    )
```

```python
import functools

import jax
import jax.numpy as jnp
from jax import lax
from jax.experimental import pallas as pl
from jax.experimental.pallas import tpu as pltpu
from jax.sharding import PartitionSpec as P

MESH = pl.DeviceIdType.MESH
F32 = jnp.float32
BF16 = jnp.bfloat16
C = 320
D = 64
ORDER = (0, 3, 1, 2)


def rms(v, gain):
    mean_sq = jnp.sum(v * v, axis=-1, keepdims=True) * (1.0 / C)
    return v * lax.rsqrt(mean_sq + 1e-06) * gain


def silu(v):
    return v / (1.0 + jnp.exp(-v))


def dot(a, b):
    return jnp.dot(a, b, preferred_element_type=F32)


def main_kernel(
    lat, g1, g2, g3, ws_h, wt_h, wq_h, wk_h, wv_h, wo_h,
    out,
    ws, wt, wq, wk, wv, wo,
    pad, send1, recv1, hid, act, hal, act2, edge, nsend, nrecv,
    qb, kb, vb, ab, asend, arecv, zsend,
    wsem, s1, r1, sx, rx, sf, rf, sn, rn, sa, ra, sz, rz, lsem,
):
    me_f = lax.axis_index("frame")
    me_r = lax.axis_index("row")
    z_hi, j = me_f // 8, me_f % 8
    x, z_lo = me_r // 4, me_r % 4
    z = z_hi * 4 + z_lo

    def dev_z(t):
        return {"frame": (t // 4) * 8 + j, "row": x * 4 + t % 4}

    def dev_x(t):
        return {"frame": me_f, "row": t * 4 + z_lo}

    def dev_j(t):
        return {"frame": z_hi * 8 + t, "row": me_r}

    bar = pltpu.get_barrier_semaphore()
    for k in range(1, 8):
        pl.semaphore_signal(bar, 1, device_id=dev_z((z + k) % 8), device_id_type=MESH)
        pl.semaphore_signal(bar, 1, device_id=dev_j((j + k) % 8), device_id_type=MESH)
    for k in (1, 3):
        pl.semaphore_signal(bar, 1, device_id=dev_x((x + k) % 4), device_id_type=MESH)

    loads = [
        pltpu.make_async_copy(a, b, wsem.at[n])
        for n, (a, b) in enumerate(
            ((ws_h, ws), (wt_h, wt), (wq_h, wq), (wk_h, wk), (wv_h, wv), (wo_h, wo))
        )
    ]
    for cp in loads:
        cp.start()

    def remote(src, dst, ss, rs, dev):
        return pltpu.make_async_remote_copy(src, dst, ss, rs, device_id=dev, device_id_type=MESH)

    def z1(c, k, i):
        t = (z + k) % 8
        return remote(send1.at[c, t, i], recv1.at[c, z, i], s1.at[c, k, i], r1.at[c, k, i], dev_z(t))

    pad[0:8] = jnp.zeros((8, 2 * C), F32)
    pad[248:256] = jnp.zeros((8, 2 * C), F32)
    for n, i in enumerate(ORDER):
        pad[8:248, 0:C] = lat[i, 0].astype(F32)
        pad[8:248, C : 2 * C] = lat[i, 1].astype(F32)
        for t in range(8):
            for c in range(2):
                lo = 7 + 30 * t + 16 * c
                send1[c, t, i] = pad[lo : lo + 16, :].astype(BF16)
        if n == 0:
            pl.semaphore_wait(bar, 16)
        for k in range(1, 8):
            z1(0, k, i).start()
        for c in range(2):
            recv1[c, z, i] = send1[c, z, i]
    for i in ORDER:
        for k in range(1, 8):
            z1(1, k, i).start()

    def hx(c, s, side):
        t = (x + (3 if side else 1)) % 4
        row = 1 if side else 8
        return remote(
            act.at[s, :, row, pl.ds(c * 16, 16)],
            hal.at[c, s, side],
            sx.at[c, s, side],
            rx.at[c, s, side],
            dev_x(t),
        )

    def hf(c, side):
        t = (j + (7 if side else 1)) % 8
        slot = 1 if side else 4
        return remote(
            act2.at[c, :, slot], edge.at[side, c], sf.at[c, side], rf.at[c, side], dev_j(t)
        )

    def activate(c, s, i):
        for k in range(1, 8):
            src = (z + 8 - k) % 8
            remote(
                send1.at[c, src, i], recv1.at[c, src, i], s1.at[c, k, i], r1.at[c, k, i], dev_z(src)
            ).wait_recv()

        def one(q, _):
            grp, zl = q // 4, q % 4
            both = recv1[c, q, i].astype(F32)
            if c == 1:
                before = recv1[0, q, i].astype(F32)
            for r in range(2):
                v = both[:, r * C : (r + 1) * C]
                kept = v
                if c == 1:
                    kept = jnp.where(tail, before[:, r * C : (r + 1) * C], v)
                hid[c, grp * 4 + i, 2 * zl + r] = kept
                act[s, grp, 2 * zl + r + 1, c * 16 : c * 16 + 16] = silu(rms(v, g1[...])).astype(BF16)
            return 0

        lax.fori_loop(0, 8, one, 0)
        hx(c, s, 0).start()
        hx(c, s, 1).start()

    tail = lax.broadcasted_iota(jnp.int32, (16, C), 0) == 15
    tail8 = lax.broadcasted_iota(jnp.int32, (8, 16, C), 1) == 15

    def convolve(c, s, i):
        for side in range(2):
            hx(c, s, side).wait_recv()
        cols = slice(c * 16, c * 16 + 16)
        top = hal[c, s, 0]
        bot = hal[c, s, 1]
        act[s, :, 0, cols] = jnp.where(x > 0, top, jnp.zeros_like(top))
        act[s, :, 9, cols] = jnp.where(x < 3, bot, jnp.zeros_like(bot))

        def mix(read):
            ys = []
            for dx in range(3):
                y = None
                for dy in range(3):
                    m = dot(read(dy), ws[dy, dx])
                    y = m if y is None else y + m
                ys.append(y)
            return ys[1] + pltpu.roll(ys[0], 1, 0) + pltpu.roll(ys[2], 255, 0)

        def close(grp, y):
            h = hid[c, grp * 4 + i] + y
            hid[c, grp * 4 + i] = h
            act2[c, grp, 1 + i] = silu(rms(h, g2[...])).astype(BF16)

        if c == 0:
            y = mix(lambda dy: act[s, :, dy : dy + 8, 0:16].reshape(256, C))
            for grp in range(2):
                close(grp, y[grp * 128 : grp * 128 + 128].reshape(8, 16, C))
        else:

            def one(grp, _):
                y = mix(lambda dy: act[s, grp, dy : dy + 8].reshape(256, C)).reshape(8, 32, C)
                close(grp, jnp.where(tail8, y[:, 0:16], y[:, 16:32]))
                return 0

            lax.fori_loop(0, 2, one, 0)
        if i == 3:
            hf(c, 0).start()
        if i == 0:
            hf(c, 1).start()

    zero = jnp.zeros((8, 16, C), BF16)
    first, last = j == 0, j == 7

    def border(c):
        hf(c, 0).wait_recv()
        hf(c, 1).wait_recv()
        act2[c, 0, 0] = jnp.where(first, zero, edge[0, c, 0])
        act2[c, 1, 0] = jnp.where(first, edge[0, c, 0], edge[0, c, 1])
        act2[c, 0, 5] = jnp.where(last, edge[1, c, 1], edge[1, c, 0])
        act2[c, 1, 5] = jnp.where(last, zero, edge[1, c, 1])

    def na(c, d):
        t = (j + d) % 8
        return remote(nsend.at[c, t], nrecv.at[c, j], sn.at[c, d], rn.at[c, d], dev_j(t))

    def temporal(c, kk):
        pair = ((j + 1 + 2 * kk) % 8, (j + 2 + 2 * kk) % 8)
        total = None
        for t in range(3):
            a = jnp.concatenate([act2[c, :, t : t + 4, r].reshape(128, C) for r in pair], axis=0)
            m = dot(a, wt[t])
            total = m if total is None else total + m
        for n, r in enumerate(pair):
            h = hid[c, :, r].reshape(128, C) + total[n * 128 : n * 128 + 128]
            hid[c, :, r] = h.reshape(8, 16, C)
            nsend[c, r] = rms(h, g3[...]).astype(BF16).reshape(8, 16, C)
            if 1 + 2 * kk + n < 8:
                na(c, 1 + 2 * kk + n).start()

    for c in range(2):
        for s, i in enumerate(ORDER):
            activate(c, s, i)
            if c == 0 and s == 1:
                loads[0].wait()
            if s > 0:
                convolve(c, s - 1, ORDER[s - 1])
        convolve(c, 3, ORDER[3])
        border(c)
        if c == 0:
            loads[1].wait()
        for kk in range(4):
            temporal(c, kk)
        nrecv[c, j] = nsend[c, j]
    for n in (2, 3, 4, 5):
        loads[n].wait()

    def project(c):
        for n in range(4):
            pair = []
            for d in (2 * n, 2 * n + 1):
                src = (j + 8 - d) % 8
                if d > 0:
                    remote(
                        nsend.at[c, src], nrecv.at[c, src], sn.at[c, d], rn.at[c, d], dev_j(src)
                    ).wait_recv()
                pair.append(src)
            a = jnp.concatenate([nrecv[c, src].reshape(128, C) for src in pair], axis=0)
            for w, buf, scale in ((wq, qb, 0.125), (wk, kb, None), (wv, vb, None)):
                y = dot(a, w[...]).astype(BF16).astype(F32)
                y = y if scale is None else y * scale
                for m, src in enumerate(pair):
                    rows = pl.ds(pl.multiple_of(c * 1024 + src * 128, 128), 128)
                    part = y[m * 128 : m * 128 + 128]
                    buf[0, rows, :] = part[:, 0:128]
                    buf[1, rows, :] = part[:, 128:256]
                    buf[2, rows, 0:D] = part[:, 256:320]

    low = lax.broadcasted_iota(jnp.int32, (64, 128), 1) < D

    def softmax_av(q, k, v):
        s = lax.dot_general(q, k, (((1,), (1,)), ((), ())), preferred_element_type=F32)
        e = jnp.exp(s - jnp.max(s, axis=-1, keepdims=True))
        tot = jnp.sum(e, axis=-1, keepdims=True)
        return dot(e.astype(BF16), v) * (1.0 / tot)

    def pixel(c, p):
        rows = pl.ds(c * 1024 + p, 64, stride=16)
        zq = jnp.zeros((64, 128), BF16)
        for hp in range(2):
            q = qb[hp, rows, :].astype(BF16)
            k = kb[hp, rows, :].astype(BF16)
            v = vb[hp, rows, :].astype(BF16)
            stacked = jnp.concatenate([jnp.where(low, q, zq), jnp.where(low, zq, q)], axis=0)
            o = softmax_av(stacked, k, v)
            ab[hp, rows, :] = jnp.where(low, o[:64], o[64:])
        q = qb[2, rows, :][:, :D].astype(BF16)
        k = kb[2, rows, :][:, :D].astype(BF16)
        v = vb[2, rows, :].astype(BF16)
        ab[2, rows, :] = softmax_av(q, k, v)

    def aa(c, d):
        t = (j + d) % 8
        return remote(asend.at[c, t], arecv.at[c, j], sa.at[c, d], ra.at[c, d], dev_j(t))

    def attend(c):
        step = 4 if c else 7

        def several(n, _):
            for m in range(step):
                pixel(c, 1 - c + n * step + m)
            return 0

        lax.fori_loop(0, 4 if c else 2, several, 0)

        def gather(t, _):
            rows = pl.ds(pl.multiple_of(c * 1024 + t * 128, 128), 128)
            full = jnp.concatenate([ab[0, rows, :], ab[1, rows, :], ab[2, rows, 0:D]], axis=-1)
            asend[c, t] = full.astype(BF16).reshape(8, 16, C)
            return 0

        lax.fori_loop(0, 8, gather, 0)
        for d in range(1, 8):
            aa(c, d).start()
        arecv[c, j] = asend[c, j]

    def z2(c, k, i):
        t = (z + k) % 8
        return remote(zsend.at[c, t, i], out.at[c, z, i], sz.at[c, k, i], rz.at[c, k, i], dev_z(t))

    def finish(c):
        for d in range(1, 8):
            src = (j + 8 - d) % 8
            remote(asend.at[c, src], arecv.at[c, src], sa.at[c, d], ra.at[c, d], dev_j(src)).wait_recv()
        for i in range(4):
            a = jnp.concatenate([arecv[c, :, g * 4 + i].reshape(128, C) for g in range(2)], axis=0)
            mixed = dot(a, wo[...])
            for g in range(2):
                res = hid[c, g * 4 + i] + mixed[g * 128 : g * 128 + 128].reshape(8, 16, C)
                for zl in range(4):
                    both = jnp.concatenate([res[2 * zl], res[2 * zl + 1]], axis=-1)
                    zsend[c, g * 4 + zl, i] = both.astype(BF16)
            for k in range(1, 8):
                z2(c, k, i).start()
        cp = pltpu.make_async_copy(zsend.at[c, z], out.at[c, z], lsem.at[c])
        cp.start()
        return cp

    project(0)
    attend(0)
    project(1)
    attend(1)
    own = [finish(0), finish(1)]

    for c in range(2):
        own[c].wait()
        for i in range(4):
            for k in range(1, 8):
                src = (z + 8 - k) % 8
                z2(c, k, i).wait_send()
                remote(
                    zsend.at[c, src, i], out.at[c, src, i], sz.at[c, k, i], rz.at[c, k, i], dev_z(src)
                ).wait_recv()
        for d in range(1, 8):
            na(c, d).wait_send()
            aa(c, d).wait_send()
    for c in range(2):
        for i in range(4):
            for k in range(1, 8):
                z1(c, k, i).wait_send()
        for side in range(2):
            for s in range(4):
                hx(c, s, side).wait_send()
            hf(c, side).wait_send()


def last_kernel(parts, out, tmp):
    tail = lax.broadcasted_iota(jnp.int32, (16, 2 * C), 0) == 15
    for t in range(8):
        right = parts[1, t, 0].astype(F32)
        tmp[t, 0:16] = jnp.where(tail, right, parts[0, t, 0].astype(F32))
        tmp[t, 16:32] = right
        both = tmp[t, 1:31, :]
        out[0, 0, 30 * t : 30 * t + 30, :] = both[:, 0:C]
        out[0, 1, 30 * t : 30 * t + 30, :] = both[:, C : 2 * C]


def local(latent, g1, ws, g2, wt, g3, wq, wk, wv, wo):
    vm = pl.BlockSpec(memory_space=pltpu.VMEM)
    anyspace = pl.BlockSpec(memory_space=pl.ANY)
    dma = pltpu.SemaphoreType.DMA
    parts = pl.pallas_call(
        main_kernel,
        out_shape=jax.ShapeDtypeStruct((2, 8, 4, 16, 2 * C), BF16),
        in_specs=[vm] * 4 + [anyspace] * 6,
        out_specs=anyspace,
        scratch_shapes=[
            pltpu.VMEM((3, 3, C, C), BF16),
            pltpu.VMEM((3, C, C), BF16),
            pltpu.VMEM((C, C), BF16),
            pltpu.VMEM((C, C), BF16),
            pltpu.VMEM((C, C), BF16),
            pltpu.VMEM((C, C), BF16),
            pltpu.VMEM((256, 2 * C), F32),
            pltpu.VMEM((2, 8, 4, 16, 2 * C), BF16),
            pltpu.VMEM((2, 8, 4, 16, 2 * C), BF16),
            pltpu.VMEM((2, 8, 8, 16, C), F32),
            pltpu.VMEM((4, 2, 10, 32, C), BF16),
            pltpu.VMEM((2, 4, 2, 2, 16, C), BF16),
            pltpu.VMEM((2, 2, 6, 8, 16, C), BF16),
            pltpu.VMEM((2, 2, 2, 8, 16, C), BF16),
            pltpu.VMEM((2, 8, 8, 16, C), BF16),
            pltpu.VMEM((2, 8, 8, 16, C), BF16),
            pltpu.VMEM((3, 2048, 128), F32),
            pltpu.VMEM((3, 2048, 128), F32),
            pltpu.VMEM((3, 2048, 128), F32),
            pltpu.VMEM((3, 2048, 128), F32),
            pltpu.VMEM((2, 8, 8, 16, C), BF16),
            pltpu.VMEM((2, 8, 8, 16, C), BF16),
            pltpu.VMEM((2, 8, 4, 16, 2 * C), BF16),
            dma((6,)),
            dma((2, 8, 4)), dma((2, 8, 4)),
            dma((2, 4, 2)), dma((2, 4, 2)),
            dma((2, 2)), dma((2, 2)),
            dma((2, 8)), dma((2, 8)),
            dma((2, 8)), dma((2, 8)),
            dma((2, 8, 4)), dma((2, 8, 4)),
            dma((2,)),
        ],
        compiler_params=pltpu.CompilerParams(
            collective_id=0, has_side_effects=True, vmem_limit_bytes=60 * 1024 * 1024
        ),
        name="block",
    )(latent, g1.reshape(1, C), g2.reshape(1, C), g3.reshape(1, C), ws, wt, wq, wk, wv, wo)
    return pl.pallas_call(
        last_kernel,
        grid=(4,),
        out_shape=jax.ShapeDtypeStruct((4, 2, 240, C), F32),
        in_specs=[pl.BlockSpec((2, 8, 1, 16, 2 * C), lambda i: (0, 0, i, 0, 0))],
        out_specs=pl.BlockSpec((1, 2, 240, C), lambda i: (i, 0, 0, 0)),
        scratch_shapes=[pltpu.VMEM((8, 32, 2 * C), F32)],
        name="assemble",
    )(parts)


def solution(mesh):
    return jax.shard_map(
        local,
        mesh=mesh,
        in_specs=(P("frame", "row", None, None),) + (P(),) * 9,
        out_specs=P("frame", "row", None, None),
        check_vma=False,
    )
```

```python
import functools

import jax
import jax.numpy as jnp
from jax import lax
from jax.experimental import pallas as pl
from jax.experimental.pallas import tpu as pltpu
from jax.sharding import PartitionSpec as P

MESH = pl.DeviceIdType.MESH
F32 = jnp.float32
BF16 = jnp.bfloat16
C = 320
D = 64
ORDER = (0, 3, 1, 2)


def rms(v, gain):
    mean_sq = jnp.sum(v * v, axis=-1, keepdims=True) * (1.0 / C)
    return v * lax.rsqrt(mean_sq + 1e-06) * gain


def silu(v):
    half = 0.5 * v
    return half + half * jnp.tanh(half)


def dot(a, b):
    return jnp.dot(a, b, preferred_element_type=F32)


def main_kernel(
    lat, g1, g2, g3, ws_h, wt_h, wq_h, wk_h, wv_h, wo_h,
    out,
    ws, wt, wq, wk, wv, wo,
    pad, send1, recv1, hid, act, hal, act2, edge, nsend, nrecv,
    qb, kb, vb, ab, asend, arecv, zsend, keep,
    wsem, s1, r1, sx, rx, sf, rf, sn, rn, sa, ra, sz, rz, lsem,
):
    me_f = lax.axis_index("frame")
    me_r = lax.axis_index("row")
    z_hi, j = me_f // 8, me_f % 8
    x, z_lo = me_r // 4, me_r % 4
    z = z_hi * 4 + z_lo

    def dev_z(t):
        return {"frame": (t // 4) * 8 + j, "row": x * 4 + t % 4}

    def dev_x(t):
        return {"frame": me_f, "row": t * 4 + z_lo}

    def dev_j(t):
        return {"frame": z_hi * 8 + t, "row": me_r}

    bar = pltpu.get_barrier_semaphore()
    for k in range(1, 8):
        pl.semaphore_signal(bar, 1, device_id=dev_z((z + k) % 8), device_id_type=MESH)
        pl.semaphore_signal(bar, 1, device_id=dev_j((j + k) % 8), device_id_type=MESH)
    for k in (1, 3):
        pl.semaphore_signal(bar, 1, device_id=dev_x((x + k) % 4), device_id_type=MESH)

    loads = [
        pltpu.make_async_copy(a, b, wsem.at[n])
        for n, (a, b) in enumerate(
            ((ws_h, ws), (wt_h, wt), (wq_h, wq), (wk_h, wk), (wv_h, wv), (wo_h, wo))
        )
    ]
    for cp in loads:
        cp.start()

    def remote(src, dst, ss, rs, dev):
        return pltpu.make_async_remote_copy(src, dst, ss, rs, device_id=dev, device_id_type=MESH)

    def z1(c, k, i):
        t = (z + k) % 8
        return remote(send1.at[c, t, i], recv1.at[c, z, i], s1.at[c, k, i], r1.at[c, k, i], dev_z(t))

    pad[0:8] = jnp.zeros((8, 2 * C), F32)
    pad[248:256] = jnp.zeros((8, 2 * C), F32)
    for n, i in enumerate(ORDER):
        pad[8:248, 0:C] = lat[i, 0].astype(F32)
        pad[8:248, C : 2 * C] = lat[i, 1].astype(F32)
        for t in range(8):
            for c in range(2):
                lo = 7 + 30 * t + 16 * c
                send1[c, t, i] = pad[lo : lo + 16, :].astype(BF16)
        if n == 0:
            pl.semaphore_wait(bar, 16)
        for k in range(1, 8):
            z1(0, k, i).start()
        for c in range(2):
            recv1[c, z, i] = send1[c, z, i]
    for i in ORDER:
        for k in range(1, 8):
            z1(1, k, i).start()

    def hx(c, s, side):
        t = (x + (3 if side else 1)) % 4
        row = 1 if side else 8
        return remote(
            act.at[s, :, row, pl.ds(c * 16, 16)],
            hal.at[c, s, side],
            sx.at[c, s, side],
            rx.at[c, s, side],
            dev_x(t),
        )

    def hf(c, side):
        t = (j + (7 if side else 1)) % 8
        slot = 1 if side else 4
        return remote(
            act2.at[c, :, slot], edge.at[side, c], sf.at[c, side], rf.at[c, side], dev_j(t)
        )

    def activate(c, s, i):
        for k in range(1, 8):
            src = (z + 8 - k) % 8
            remote(
                send1.at[c, src, i], recv1.at[c, src, i], s1.at[c, k, i], r1.at[c, k, i], dev_z(src)
            ).wait_recv()

        def one(q, _):
            grp, zl = q // 4, q % 4
            both = recv1[c, q, i].astype(F32)
            if c == 1:
                before = recv1[0, q, i].astype(F32)
            for r in range(2):
                v = both[:, r * C : (r + 1) * C]
                kept = v
                if c == 1:
                    kept = jnp.where(tail, before[:, r * C : (r + 1) * C], v)
                hid[c, grp * 4 + i, 2 * zl + r] = kept
                act[s, grp, 2 * zl + r + 1, c * 16 : c * 16 + 16] = silu(rms(v, g1[...])).astype(BF16)
            return 0

        lax.fori_loop(0, 8, one, 0)
        hx(c, s, 0).start()
        hx(c, s, 1).start()

    tail = lax.broadcasted_iota(jnp.int32, (16, C), 0) == 15

    def convolve(c, s, i):
        for side in range(2):
            hx(c, s, side).wait_recv()
        cols = slice(c * 16, c * 16 + 16)
        top = hal[c, s, 0]
        bot = hal[c, s, 1]
        act[s, :, 0, cols] = jnp.where(x > 0, top, jnp.zeros_like(top))
        act[s, :, 9, cols] = jnp.where(x < 3, bot, jnp.zeros_like(bot))

        def mix(read):
            ys = []
            for dx in range(3):
                y = None
                for dy in range(3):
                    m = dot(read(dy), ws[dy, dx])
                    y = m if y is None else y + m
                ys.append(y)
            return ys

        def close(grp, y):
            h = hid[c, grp * 4 + i] + y
            hid[c, grp * 4 + i] = h
            act2[c, grp, 1 + i] = silu(rms(h, g2[...])).astype(BF16)

        y0, y1, y2 = mix(lambda dy: act[s, :, dy : dy + 8, cols].reshape(256, C))
        if c == 0:
            part = y1 + pltpu.roll(y0, 1, 0)
            keep[s, 0] = y0
            keep[s, 1] = part
            y = part + pltpu.roll(y2, 255, 0)
        else:
            slot = lax.broadcasted_iota(jnp.int32, (256, C), 0) % 16
            left = jnp.where(slot == 0, pltpu.roll(keep[s, 0], 241, 0), pltpu.roll(y0, 1, 0))
            y = y1 + left + pltpu.roll(y2, 255, 0)
            y = jnp.where(slot == 15, keep[s, 1] + pltpu.roll(y2, 15, 0), y)
        for grp in range(2):
            close(grp, y[grp * 128 : grp * 128 + 128].reshape(8, 16, C))
        if i == 3:
            hf(c, 0).start()
        if i == 0:
            hf(c, 1).start()

    zero = jnp.zeros((8, 16, C), BF16)
    first, last = j == 0, j == 7

    def border(c):
        hf(c, 0).wait_recv()
        hf(c, 1).wait_recv()
        act2[c, 0, 0] = jnp.where(first, zero, edge[0, c, 0])
        act2[c, 1, 0] = jnp.where(first, edge[0, c, 0], edge[0, c, 1])
        act2[c, 0, 5] = jnp.where(last, edge[1, c, 1], edge[1, c, 0])
        act2[c, 1, 5] = jnp.where(last, zero, edge[1, c, 1])

    def na(c, d):
        t = (j + d) % 8
        return remote(nsend.at[c, t], nrecv.at[c, j], sn.at[c, d], rn.at[c, d], dev_j(t))

    def temporal(c, kk):
        pair = ((j + 1 + 2 * kk) % 8, (j + 2 + 2 * kk) % 8)
        total = None
        for t in range(3):
            a = jnp.concatenate([act2[c, :, t : t + 4, r].reshape(128, C) for r in pair], axis=0)
            m = dot(a, wt[t])
            total = m if total is None else total + m
        for n, r in enumerate(pair):
            h = hid[c, :, r].reshape(128, C) + total[n * 128 : n * 128 + 128]
            hid[c, :, r] = h.reshape(8, 16, C)
            nsend[c, r] = rms(h, g3[...]).astype(BF16).reshape(8, 16, C)
            if 1 + 2 * kk + n < 8:
                na(c, 1 + 2 * kk + n).start()

    for c in range(2):
        for s, i in enumerate(ORDER):
            activate(c, s, i)
            if c == 0 and s == 1:
                loads[0].wait()
            if s > 0:
                convolve(c, s - 1, ORDER[s - 1])
        convolve(c, 3, ORDER[3])
        border(c)
        if c == 0:
            loads[1].wait()
        for kk in range(4):
            temporal(c, kk)
        nrecv[c, j] = nsend[c, j]
    for n in (2, 3, 4, 5):
        loads[n].wait()

    def project(c):
        for n in range(4):
            pair = []
            for d in (2 * n, 2 * n + 1):
                src = (j + 8 - d) % 8
                if d > 0:
                    remote(
                        nsend.at[c, src], nrecv.at[c, src], sn.at[c, d], rn.at[c, d], dev_j(src)
                    ).wait_recv()
                pair.append(src)
            a = jnp.concatenate([nrecv[c, src].reshape(128, C) for src in pair], axis=0)
            for w, buf, scale in ((wq, qb, 0.125), (wk, kb, None), (wv, vb, None)):
                y = dot(a, w[...]).astype(BF16).astype(F32)
                y = y if scale is None else y * scale
                for m, src in enumerate(pair):
                    rows = pl.ds(pl.multiple_of(c * 1024 + src * 128, 128), 128)
                    part = y[m * 128 : m * 128 + 128]
                    buf[0, rows, :] = part[:, 0:128]
                    buf[1, rows, :] = part[:, 128:256]
                    buf[2, rows, 0:D] = part[:, 256:320]

    low = lax.broadcasted_iota(jnp.int32, (64, 128), 1) < D

    def softmax_av(q, k, v):
        s = lax.dot_general(q, k, (((1,), (1,)), ((), ())), preferred_element_type=F32)
        e = jnp.exp(s - jnp.max(s, axis=-1, keepdims=True))
        tot = jnp.sum(e, axis=-1, keepdims=True)
        return dot(e.astype(BF16), v) * (1.0 / tot)

    def pixel(c, p):
        rows = pl.ds(c * 1024 + p, 64, stride=16)
        zq = jnp.zeros((64, 128), BF16)
        for hp in range(2):
            q = qb[hp, rows, :].astype(BF16)
            k = kb[hp, rows, :].astype(BF16)
            v = vb[hp, rows, :].astype(BF16)
            stacked = jnp.concatenate([jnp.where(low, q, zq), jnp.where(low, zq, q)], axis=0)
            o = softmax_av(stacked, k, v)
            ab[hp, rows, :] = jnp.where(low, o[:64], o[64:])
        q = qb[2, rows, :][:, :D].astype(BF16)
        k = kb[2, rows, :][:, :D].astype(BF16)
        v = vb[2, rows, :].astype(BF16)
        ab[2, rows, :] = softmax_av(q, k, v)

    def aa(c, d):
        t = (j + d) % 8
        return remote(asend.at[c, t], arecv.at[c, j], sa.at[c, d], ra.at[c, d], dev_j(t))

    def attend(c):
        step = 4 if c else 7

        def several(n, _):
            for m in range(step):
                pixel(c, 1 - c + n * step + m)
            return 0

        lax.fori_loop(0, 4 if c else 2, several, 0)

        def gather(t, _):
            rows = pl.ds(pl.multiple_of(c * 1024 + t * 128, 128), 128)
            full = jnp.concatenate([ab[0, rows, :], ab[1, rows, :], ab[2, rows, 0:D]], axis=-1)
            asend[c, t] = full.astype(BF16).reshape(8, 16, C)
            return 0

        lax.fori_loop(0, 8, gather, 0)
        for d in range(1, 8):
            aa(c, d).start()
        arecv[c, j] = asend[c, j]

    def z2(c, k, i):
        t = (z + k) % 8
        return remote(zsend.at[c, t, i], out.at[c, z, i], sz.at[c, k, i], rz.at[c, k, i], dev_z(t))

    def finish(c):
        for d in range(1, 8):
            src = (j + 8 - d) % 8
            remote(asend.at[c, src], arecv.at[c, src], sa.at[c, d], ra.at[c, d], dev_j(src)).wait_recv()
        for i in range(4):
            a = jnp.concatenate([arecv[c, :, g * 4 + i].reshape(128, C) for g in range(2)], axis=0)
            mixed = dot(a, wo[...])
            for g in range(2):
                res = hid[c, g * 4 + i] + mixed[g * 128 : g * 128 + 128].reshape(8, 16, C)
                for zl in range(4):
                    both = jnp.concatenate([res[2 * zl], res[2 * zl + 1]], axis=-1)
                    zsend[c, g * 4 + zl, i] = both.astype(BF16)
            for k in range(1, 8):
                z2(c, k, i).start()
        cp = pltpu.make_async_copy(zsend.at[c, z], out.at[c, z], lsem.at[c])
        cp.start()
        return cp

    project(0)
    attend(0)
    project(1)
    attend(1)
    own = [finish(0), finish(1)]

    for c in range(2):
        own[c].wait()
        for i in range(4):
            for k in range(1, 8):
                src = (z + 8 - k) % 8
                z2(c, k, i).wait_send()
                remote(
                    zsend.at[c, src, i], out.at[c, src, i], sz.at[c, k, i], rz.at[c, k, i], dev_z(src)
                ).wait_recv()
        for d in range(1, 8):
            na(c, d).wait_send()
            aa(c, d).wait_send()
    for c in range(2):
        for i in range(4):
            for k in range(1, 8):
                z1(c, k, i).wait_send()
        for side in range(2):
            for s in range(4):
                hx(c, s, side).wait_send()
            hf(c, side).wait_send()


def last_kernel(parts, out, tmp):
    tail = lax.broadcasted_iota(jnp.int32, (16, 2 * C), 0) == 15
    for t in range(8):
        right = parts[1, t, 0].astype(F32)
        tmp[t, 0:16] = jnp.where(tail, right, parts[0, t, 0].astype(F32))
        tmp[t, 16:32] = right
        both = tmp[t, 1:31, :]
        out[0, 0, 30 * t : 30 * t + 30, :] = both[:, 0:C]
        out[0, 1, 30 * t : 30 * t + 30, :] = both[:, C : 2 * C]


def local(latent, g1, ws, g2, wt, g3, wq, wk, wv, wo):
    vm = pl.BlockSpec(memory_space=pltpu.VMEM)
    anyspace = pl.BlockSpec(memory_space=pl.ANY)
    dma = pltpu.SemaphoreType.DMA
    parts = pl.pallas_call(
        main_kernel,
        out_shape=jax.ShapeDtypeStruct((2, 8, 4, 16, 2 * C), BF16),
        in_specs=[vm] * 4 + [anyspace] * 6,
        out_specs=anyspace,
        scratch_shapes=[
            pltpu.VMEM((3, 3, C, C), BF16),
            pltpu.VMEM((3, C, C), BF16),
            pltpu.VMEM((C, C), BF16),
            pltpu.VMEM((C, C), BF16),
            pltpu.VMEM((C, C), BF16),
            pltpu.VMEM((C, C), BF16),
            pltpu.VMEM((256, 2 * C), F32),
            pltpu.VMEM((2, 8, 4, 16, 2 * C), BF16),
            pltpu.VMEM((2, 8, 4, 16, 2 * C), BF16),
            pltpu.VMEM((2, 8, 8, 16, C), F32),
            pltpu.VMEM((4, 2, 10, 32, C), BF16),
            pltpu.VMEM((2, 4, 2, 2, 16, C), BF16),
            pltpu.VMEM((2, 2, 6, 8, 16, C), BF16),
            pltpu.VMEM((2, 2, 2, 8, 16, C), BF16),
            pltpu.VMEM((2, 8, 8, 16, C), BF16),
            pltpu.VMEM((2, 8, 8, 16, C), BF16),
            pltpu.VMEM((3, 2048, 128), F32),
            pltpu.VMEM((3, 2048, 128), F32),
            pltpu.VMEM((3, 2048, 128), F32),
            pltpu.VMEM((3, 2048, 128), F32),
            pltpu.VMEM((2, 8, 8, 16, C), BF16),
            pltpu.VMEM((2, 8, 8, 16, C), BF16),
            pltpu.VMEM((2, 8, 4, 16, 2 * C), BF16),
            pltpu.VMEM((4, 2, 256, C), F32),
            dma((6,)),
            dma((2, 8, 4)), dma((2, 8, 4)),
            dma((2, 4, 2)), dma((2, 4, 2)),
            dma((2, 2)), dma((2, 2)),
            dma((2, 8)), dma((2, 8)),
            dma((2, 8)), dma((2, 8)),
            dma((2, 8, 4)), dma((2, 8, 4)),
            dma((2,)),
        ],
        compiler_params=pltpu.CompilerParams(
            collective_id=0, has_side_effects=True, vmem_limit_bytes=60 * 1024 * 1024
        ),
        name="block",
    )(latent, g1.reshape(1, C), g2.reshape(1, C), g3.reshape(1, C), ws, wt, wq, wk, wv, wo)
    return pl.pallas_call(
        last_kernel,
        grid=(4,),
        out_shape=jax.ShapeDtypeStruct((4, 2, 240, C), F32),
        in_specs=[pl.BlockSpec((2, 8, 1, 16, 2 * C), lambda i: (0, 0, i, 0, 0))],
        out_specs=pl.BlockSpec((1, 2, 240, C), lambda i: (i, 0, 0, 0)),
        scratch_shapes=[pltpu.VMEM((8, 32, 2 * C), F32)],
        name="assemble",
    )(parts)


def solution(mesh):
    return jax.shard_map(
        local,
        mesh=mesh,
        in_specs=(P("frame", "row", None, None),) + (P(),) * 9,
        out_specs=P("frame", "row", None, None),
        check_vma=False,
    )
```

```python
import functools

import jax
import jax.numpy as jnp
from jax import lax
from jax.experimental import pallas as pl
from jax.experimental.pallas import tpu as pltpu
from jax.sharding import PartitionSpec as P

MESH = pl.DeviceIdType.MESH
F32 = jnp.float32
BF16 = jnp.bfloat16
C = 320
D = 64
ORDER = (0, 3, 1, 2)


def rms(v, gain):
    mean_sq = jnp.sum(v * v, axis=-1, keepdims=True) * (1.0 / C)
    return v * lax.rsqrt(mean_sq + 1e-06) * gain


def silu(v):
    half = 0.5 * v
    return half + half * jnp.tanh(half)


def dot(a, b):
    return jnp.dot(a, b, preferred_element_type=F32)


def main_kernel(
    lat, g1, g2, g3, ws_h, wt_h, wq_h, wk_h, wv_h, wo_h,
    out,
    ws, wt, wq, wk, wv, wo,
    pad, send1, recv1, hid, act, hal, act2, edge, nsend, nrecv,
    qb, kb, vb, ab, asend, arecv, zsend, keep,
    wsem, s1, r1, sx, rx, sf, rf, sn, rn, sa, ra, sz, rz, lsem,
):
    me_f = lax.axis_index("frame")
    me_r = lax.axis_index("row")
    z_hi, j = me_f // 8, me_f % 8
    x, z_lo = me_r // 4, me_r % 4
    z = z_hi * 4 + z_lo

    def dev_z(t):
        return {"frame": (t // 4) * 8 + j, "row": x * 4 + t % 4}

    def dev_x(t):
        return {"frame": me_f, "row": t * 4 + z_lo}

    def dev_j(t):
        return {"frame": z_hi * 8 + t, "row": me_r}

    bar = pltpu.get_barrier_semaphore()
    for k in range(1, 8):
        pl.semaphore_signal(bar, 1, device_id=dev_z((z + k) % 8), device_id_type=MESH)
        pl.semaphore_signal(bar, 1, device_id=dev_j((j + k) % 8), device_id_type=MESH)
    for k in (1, 3):
        pl.semaphore_signal(bar, 1, device_id=dev_x((x + k) % 4), device_id_type=MESH)

    loads = [
        pltpu.make_async_copy(a, b, wsem.at[n])
        for n, (a, b) in enumerate(
            ((ws_h, ws), (wt_h, wt), (wq_h, wq), (wk_h, wk), (wv_h, wv), (wo_h, wo))
        )
    ]
    for cp in loads:
        cp.start()

    def remote(src, dst, ss, rs, dev):
        return pltpu.make_async_remote_copy(src, dst, ss, rs, device_id=dev, device_id_type=MESH)

    def z1(c, k, i):
        t = (z + k) % 8
        return remote(send1.at[c, t, i], recv1.at[c, z, i], s1.at[c, k, i], r1.at[c, k, i], dev_z(t))

    pad[0:8] = jnp.zeros((8, 2 * C), F32)
    pad[248:256] = jnp.zeros((8, 2 * C), F32)
    for n, i in enumerate(ORDER):
        pad[8:248, 0:C] = lat[i, 0].astype(F32)
        pad[8:248, C : 2 * C] = lat[i, 1].astype(F32)
        for t in range(8):
            for c in range(2):
                lo = 7 + 30 * t + 16 * c
                send1[c, t, i] = pad[lo : lo + 16, :].astype(BF16)
        if n == 0:
            pl.semaphore_wait(bar, 16)
        for k in range(1, 8):
            z1(0, k, i).start()
        for c in range(2):
            recv1[c, z, i] = send1[c, z, i]
    for i in ORDER:
        for k in range(1, 8):
            z1(1, k, i).start()

    def hx(c, s, side):
        t = (x + (3 if side else 1)) % 4
        row = 1 if side else 8
        return remote(
            act.at[s, :, row, pl.ds(c * 16, 16)],
            hal.at[c, s, side],
            sx.at[c, s, side],
            rx.at[c, s, side],
            dev_x(t),
        )

    def hf(c, side):
        t = (j + (7 if side else 1)) % 8
        slot = 1 if side else 4
        return remote(
            act2.at[c, :, slot], edge.at[side, c], sf.at[c, side], rf.at[c, side], dev_j(t)
        )

    def activate(c, s, i):
        for k in range(1, 8):
            src = (z + 8 - k) % 8
            remote(
                send1.at[c, src, i], recv1.at[c, src, i], s1.at[c, k, i], r1.at[c, k, i], dev_z(src)
            ).wait_recv()

        def one(q, _):
            grp, zl = q // 4, q % 4
            both = recv1[c, q, i].astype(F32)
            if c == 1:
                before = recv1[0, q, i].astype(F32)
            for r in range(2):
                v = both[:, r * C : (r + 1) * C]
                kept = v
                if c == 1:
                    kept = jnp.where(tail, before[:, r * C : (r + 1) * C], v)
                hid[c, grp * 4 + i, 2 * zl + r] = kept
                act[s, grp, 2 * zl + r + 1, c * 16 : c * 16 + 16] = silu(rms(v, g1[...])).astype(BF16)
            return 0

        lax.fori_loop(0, 8, one, 0)
        hx(c, s, 0).start()
        hx(c, s, 1).start()

    tail = lax.broadcasted_iota(jnp.int32, (16, C), 0) == 15

    def convolve(c, s, i):
        for side in range(2):
            hx(c, s, side).wait_recv()
        cols = slice(c * 16, c * 16 + 16)
        top = hal[c, s, 0]
        bot = hal[c, s, 1]
        act[s, :, 0, cols] = jnp.where(x > 0, top, jnp.zeros_like(top))
        act[s, :, 9, cols] = jnp.where(x < 3, bot, jnp.zeros_like(bot))

        def mix(read):
            ys = []
            for dx in range(3):
                y = None
                for dy in range(3):
                    m = dot(read(dy), ws[dy, dx])
                    y = m if y is None else y + m
                ys.append(y)
            return ys

        def close(grp, y):
            h = hid[c, grp * 4 + i] + y
            hid[c, grp * 4 + i] = h
            act2[c, grp, 1 + i] = silu(rms(h, g2[...])).astype(BF16)

        y0, y1, y2 = mix(lambda dy: act[s, :, dy : dy + 8, cols].reshape(256, C))
        if c == 0:
            part = y1 + pltpu.roll(y0, 1, 0)
            keep[s, 0] = y0
            keep[s, 1] = part
            y = part + pltpu.roll(y2, 255, 0)
        else:
            slot = lax.broadcasted_iota(jnp.int32, (256, C), 0) % 16
            left = jnp.where(slot == 0, pltpu.roll(keep[s, 0], 241, 0), pltpu.roll(y0, 1, 0))
            y = y1 + left + pltpu.roll(y2, 255, 0)
            y = jnp.where(slot == 15, keep[s, 1] + pltpu.roll(y2, 15, 0), y)
        for grp in range(2):
            close(grp, y[grp * 128 : grp * 128 + 128].reshape(8, 16, C))
        if i == 3:
            hf(c, 0).start()
        if i == 0:
            hf(c, 1).start()

    zero = jnp.zeros((8, 16, C), BF16)
    first, last = j == 0, j == 7

    def border(c):
        hf(c, 0).wait_recv()
        hf(c, 1).wait_recv()
        act2[c, 0, 0] = jnp.where(first, zero, edge[0, c, 0])
        act2[c, 1, 0] = jnp.where(first, edge[0, c, 0], edge[0, c, 1])
        act2[c, 0, 5] = jnp.where(last, edge[1, c, 1], edge[1, c, 0])
        act2[c, 1, 5] = jnp.where(last, zero, edge[1, c, 1])

    def na(c, d):
        t = (j + d) % 8
        return remote(nsend.at[c, t], nrecv.at[c, j], sn.at[c, d], rn.at[c, d], dev_j(t))

    def temporal(c, kk):
        pair = ((j + 1 + 2 * kk) % 8, (j + 2 + 2 * kk) % 8)
        total = None
        for t in range(3):
            a = jnp.concatenate([act2[c, :, t : t + 4, r].reshape(128, C) for r in pair], axis=0)
            m = dot(a, wt[t])
            total = m if total is None else total + m
        for n, r in enumerate(pair):
            h = hid[c, :, r].reshape(128, C) + total[n * 128 : n * 128 + 128]
            hid[c, :, r] = h.reshape(8, 16, C)
            nsend[c, r] = rms(h, g3[...]).astype(BF16).reshape(8, 16, C)
            if 1 + 2 * kk + n < 8:
                na(c, 1 + 2 * kk + n).start()

    def project(c):
        for n in range(4):
            pair = []
            for d in (2 * n, 2 * n + 1):
                src = (j + 8 - d) % 8
                if d > 0:
                    remote(
                        nsend.at[c, src], nrecv.at[c, src], sn.at[c, d], rn.at[c, d], dev_j(src)
                    ).wait_recv()
                pair.append(src)
            a = jnp.concatenate([nrecv[c, src].reshape(128, C) for src in pair], axis=0)
            for w, buf, scale in ((wq, qb, 0.125), (wk, kb, None), (wv, vb, None)):
                y = dot(a, w[...]).astype(BF16).astype(F32)
                y = y if scale is None else y * scale
                for m, src in enumerate(pair):
                    rows = pl.ds(pl.multiple_of(c * 1024 + src * 128, 128), 128)
                    part = y[m * 128 : m * 128 + 128]
                    buf[0, rows, :] = part[:, 0:128]
                    buf[1, rows, :] = part[:, 128:256]
                    buf[2, rows, 0:D] = part[:, 256:320]

    low = lax.broadcasted_iota(jnp.int32, (64, 128), 1) < D

    def softmax_av(q, k, v):
        s = lax.dot_general(q, k, (((1,), (1,)), ((), ())), preferred_element_type=F32)
        e = jnp.exp(s - jnp.max(s, axis=-1, keepdims=True))
        tot = jnp.sum(e, axis=-1, keepdims=True)
        return dot(e.astype(BF16), v) * (1.0 / tot)

    def pixel(c, p):
        rows = pl.ds(c * 1024 + p, 64, stride=16)
        zq = jnp.zeros((64, 128), BF16)
        for hp in range(2):
            q = qb[hp, rows, :].astype(BF16)
            k = kb[hp, rows, :].astype(BF16)
            v = vb[hp, rows, :].astype(BF16)
            stacked = jnp.concatenate([jnp.where(low, q, zq), jnp.where(low, zq, q)], axis=0)
            o = softmax_av(stacked, k, v)
            ab[hp, rows, :] = jnp.where(low, o[:64], o[64:])
        q = qb[2, rows, :][:, :D].astype(BF16)
        k = kb[2, rows, :][:, :D].astype(BF16)
        v = vb[2, rows, :].astype(BF16)
        ab[2, rows, :] = softmax_av(q, k, v)

    def aa(c, d):
        t = (j + d) % 8
        return remote(asend.at[c, t], arecv.at[c, j], sa.at[c, d], ra.at[c, d], dev_j(t))

    def attend(c):
        step = 4 if c else 7

        def several(n, _):
            for m in range(step):
                pixel(c, 1 - c + n * step + m)
            return 0

        lax.fori_loop(0, 4 if c else 2, several, 0)

        def gather(t, _):
            rows = pl.ds(pl.multiple_of(c * 1024 + t * 128, 128), 128)
            full = jnp.concatenate([ab[0, rows, :], ab[1, rows, :], ab[2, rows, 0:D]], axis=-1)
            asend[c, t] = full.astype(BF16).reshape(8, 16, C)
            return 0

        lax.fori_loop(0, 8, gather, 0)
        for d in range(1, 8):
            aa(c, d).start()
        arecv[c, j] = asend[c, j]

    def z2(c, k, i):
        t = (z + k) % 8
        return remote(zsend.at[c, t, i], out.at[c, z, i], sz.at[c, k, i], rz.at[c, k, i], dev_z(t))

    def finish(c):
        for d in range(1, 8):
            src = (j + 8 - d) % 8
            remote(asend.at[c, src], arecv.at[c, src], sa.at[c, d], ra.at[c, d], dev_j(src)).wait_recv()
        for i in range(4):
            a = jnp.concatenate([arecv[c, :, g * 4 + i].reshape(128, C) for g in range(2)], axis=0)
            mixed = dot(a, wo[...])
            for g in range(2):
                res = hid[c, g * 4 + i] + mixed[g * 128 : g * 128 + 128].reshape(8, 16, C)
                for zl in range(4):
                    both = jnp.concatenate([res[2 * zl], res[2 * zl + 1]], axis=-1)
                    zsend[c, g * 4 + zl, i] = both.astype(BF16)
            for k in range(1, 8):
                z2(c, k, i).start()
        cp = pltpu.make_async_copy(zsend.at[c, z], out.at[c, z], lsem.at[c])
        cp.start()
        return cp

    for c in range(2):
        for s, i in enumerate(ORDER):
            activate(c, s, i)
            if c == 0 and s == 1:
                loads[0].wait()
            if s > 0:
                convolve(c, s - 1, ORDER[s - 1])
        convolve(c, 3, ORDER[3])
        if c == 1:
            for n in (2, 3, 4, 5):
                loads[n].wait()
            project(0)
            attend(0)
        border(c)
        if c == 0:
            loads[1].wait()
        for kk in range(4):
            temporal(c, kk)
        nrecv[c, j] = nsend[c, j]

    own = [finish(0)]
    project(1)
    attend(1)
    own.append(finish(1))

    for c in range(2):
        own[c].wait()
        for i in range(4):
            for k in range(1, 8):
                src = (z + 8 - k) % 8
                z2(c, k, i).wait_send()
                remote(
                    zsend.at[c, src, i], out.at[c, src, i], sz.at[c, k, i], rz.at[c, k, i], dev_z(src)
                ).wait_recv()
        for d in range(1, 8):
            na(c, d).wait_send()
            aa(c, d).wait_send()
    for c in range(2):
        for i in range(4):
            for k in range(1, 8):
                z1(c, k, i).wait_send()
        for side in range(2):
            for s in range(4):
                hx(c, s, side).wait_send()
            hf(c, side).wait_send()


def last_kernel(parts, out, tmp):
    tail = lax.broadcasted_iota(jnp.int32, (16, 2 * C), 0) == 15
    for t in range(8):
        right = parts[1, t, 0].astype(F32)
        tmp[t, 0:16] = jnp.where(tail, right, parts[0, t, 0].astype(F32))
        tmp[t, 16:32] = right
        both = tmp[t, 1:31, :]
        out[0, 0, 30 * t : 30 * t + 30, :] = both[:, 0:C]
        out[0, 1, 30 * t : 30 * t + 30, :] = both[:, C : 2 * C]


def local(latent, g1, ws, g2, wt, g3, wq, wk, wv, wo):
    vm = pl.BlockSpec(memory_space=pltpu.VMEM)
    anyspace = pl.BlockSpec(memory_space=pl.ANY)
    dma = pltpu.SemaphoreType.DMA
    parts = pl.pallas_call(
        main_kernel,
        out_shape=jax.ShapeDtypeStruct((2, 8, 4, 16, 2 * C), BF16),
        in_specs=[vm] * 4 + [anyspace] * 6,
        out_specs=anyspace,
        scratch_shapes=[
            pltpu.VMEM((3, 3, C, C), BF16),
            pltpu.VMEM((3, C, C), BF16),
            pltpu.VMEM((C, C), BF16),
            pltpu.VMEM((C, C), BF16),
            pltpu.VMEM((C, C), BF16),
            pltpu.VMEM((C, C), BF16),
            pltpu.VMEM((256, 2 * C), F32),
            pltpu.VMEM((2, 8, 4, 16, 2 * C), BF16),
            pltpu.VMEM((2, 8, 4, 16, 2 * C), BF16),
            pltpu.VMEM((2, 8, 8, 16, C), F32),
            pltpu.VMEM((4, 2, 10, 32, C), BF16),
            pltpu.VMEM((2, 4, 2, 2, 16, C), BF16),
            pltpu.VMEM((2, 2, 6, 8, 16, C), BF16),
            pltpu.VMEM((2, 2, 2, 8, 16, C), BF16),
            pltpu.VMEM((2, 8, 8, 16, C), BF16),
            pltpu.VMEM((2, 8, 8, 16, C), BF16),
            pltpu.VMEM((3, 2048, 128), F32),
            pltpu.VMEM((3, 2048, 128), F32),
            pltpu.VMEM((3, 2048, 128), F32),
            pltpu.VMEM((3, 2048, 128), F32),
            pltpu.VMEM((2, 8, 8, 16, C), BF16),
            pltpu.VMEM((2, 8, 8, 16, C), BF16),
            pltpu.VMEM((2, 8, 4, 16, 2 * C), BF16),
            pltpu.VMEM((4, 2, 256, C), F32),
            dma((6,)),
            dma((2, 8, 4)), dma((2, 8, 4)),
            dma((2, 4, 2)), dma((2, 4, 2)),
            dma((2, 2)), dma((2, 2)),
            dma((2, 8)), dma((2, 8)),
            dma((2, 8)), dma((2, 8)),
            dma((2, 8, 4)), dma((2, 8, 4)),
            dma((2,)),
        ],
        compiler_params=pltpu.CompilerParams(
            collective_id=0, has_side_effects=True, vmem_limit_bytes=60 * 1024 * 1024
        ),
        name="block",
    )(latent, g1.reshape(1, C), g2.reshape(1, C), g3.reshape(1, C), ws, wt, wq, wk, wv, wo)
    return pl.pallas_call(
        last_kernel,
        grid=(4,),
        out_shape=jax.ShapeDtypeStruct((4, 2, 240, C), F32),
        in_specs=[pl.BlockSpec((2, 8, 1, 16, 2 * C), lambda i: (0, 0, i, 0, 0))],
        out_specs=pl.BlockSpec((1, 2, 240, C), lambda i: (i, 0, 0, 0)),
        scratch_shapes=[pltpu.VMEM((8, 32, 2 * C), F32)],
        name="assemble",
    )(parts)


def solution(mesh):
    return jax.shard_map(
        local,
        mesh=mesh,
        in_specs=(P("frame", "row", None, None),) + (P(),) * 9,
        out_specs=P("frame", "row", None, None),
        check_vma=False,
    )
```
